512 devices in a mesh: rows: 64 (over y, z), depth: 8 (over x, core).
Axes of the slice: x: 4, y: 4, z: 16, core: 2. Of those that a mesh axis runs over, the one named last changes fastest.
Arguments:
- grid_values: float32 [4, 256, 512, 512], P(None, 'depth', 'rows'), may hold values from -4 to 550, as said below
- image_grad: float32 [3, 512, 512], P(None, 'rows', 'depth'), may hold values from -384 to 384
Outputs:
- grid_grad: float32 [4, 256, 512, 512], P(None, 'depth', 'rows')
The draws below stay inside these ranges and needn't reach their ends.
Inputs may be any that keep to these rules, and one draw needn't show every extreme that they name: `grid_values`: channel 0 holds nonnegative densities; channels 1 to 3 hold colors within -4 to 4.
All inputs are finite; a program needn't handle non-finite values.
Results may differ from the reference program's by a relative error of at most 0.000029.
Values sent between devices are 32-bit elements; how exact they have to be, the bound alone decides.
A program may use at most 64 MiB of HBM per device.

```python
import math
import jax
import jax.numpy as jnp
from jax import lax

IMAGE_COLUMNS = 512
IMAGE_ROWS = 512
RAY_DEPTH_CELLS = 256


def draw_grid_values(key, part):
    random_keys = jax.random.split(key, 5)
    pixel_scale = jnp.exp(jax.random.uniform(random_keys[0], (IMAGE_ROWS, IMAGE_COLUMNS), jnp.float32, math.log(0.5), math.log(25.0)))
    cell_factor = jax.random.uniform(random_keys[1], (RAY_DEPTH_CELLS, IMAGE_ROWS, IMAGE_COLUMNS), jnp.float32, 0.5, 1.5)
    density_field = pixel_scale[None] * cell_factor
    spike_cells = jax.random.randint(random_keys[2], (2, IMAGE_ROWS, IMAGE_COLUMNS), 0, RAY_DEPTH_CELLS)
    spike_amount = jax.random.uniform(random_keys[3], (2, IMAGE_ROWS, IMAGE_COLUMNS), jnp.float32, 0.22, 0.69)
    depth_position_index = jnp.arange(RAY_DEPTH_CELLS, dtype=jnp.int32)[:, None, None]
    for chosen_cells in range(2):
        spike_hit = (depth_position_index == spike_cells[chosen_cells][None]).astype(jnp.float32)
        density_field = density_field + spike_hit * spike_amount[chosen_cells][None] * RAY_DEPTH_CELLS
    colors = jax.random.truncated_normal(random_keys[4], -4.0, 4.0, (3, RAY_DEPTH_CELLS, IMAGE_ROWS, IMAGE_COLUMNS), jnp.float32)
    return jnp.concatenate([density_field[None], colors], axis=0).astype(jnp.float32)


def block_scale(rng, extent, cuts, least, top_value):
    gain, own = 1.0, jax.random.fold_in(rng, 6)
    for position, shards_of in cuts:
        draws = jnp.exp(jax.random.uniform(jax.random.fold_in(own, position), (shards_of,), jnp.float32, least / len(cuts), top_value / len(cuts)))
        gain = gain * jnp.repeat(draws, extent[position] // shards_of).reshape([-1 if axis == position else 1 for axis in range(len(extent))])
    return gain


def bell_draw(own_key, extent, spread, bound, pieces=(), kind=jnp.bfloat16):
    drawn = spread * jax.random.normal(own_key, extent, jnp.float32)
    if pieces:
        drawn = drawn * block_scale(own_key, extent, pieces, -0.22, 0.18)
    return jnp.clip(drawn, -bound, bound).astype(kind)


def setup_inputs(seed: int = 0) -> dict:
    key_list = jax.random.split(jax.random.key(seed), 3)
    return {
        "grid_values": draw_grid_values(jax.random.fold_in(key_list[2], 71), 0),
        "image_grad": bell_draw(key_list[1], (3, IMAGE_ROWS, IMAGE_COLUMNS), 64.0, 384.0, ((1, 64), (2, 8)), jnp.float32),
    }


SMOOTH = 0.01
TV_WEIGHT = 0.05

def slope_of(difference):
    return difference / jnp.sqrt(difference * difference + SMOOTH)

def tv_along(values, axis):
    slopes = slope_of(jnp.diff(values, axis=axis))
    shape = list(slopes.shape)
    shape[axis] = 1
    zeros = jnp.zeros(shape, jnp.float32)
    return jnp.concatenate([zeros, slopes], axis) - jnp.concatenate([slopes, zeros], axis)

def reference(grid_values, image_grad):
    density_field = grid_values[0]
    colors = grid_values[1:]
    optical = density_field / RAY_DEPTH_CELLS
    before = jnp.cumsum(optical, axis=0) - optical
    transmit = jnp.exp(-before)
    survive = jnp.exp(-optical)
    weight = transmit * (1.0 - survive)
    shaded = lax.optimization_barrier(jnp.sum(image_grad[:, None] * colors, axis=0))
    emitted = weight * shaded
    later = jnp.cumsum(emitted[::-1], axis=0)[::-1] - emitted
    grad_density = (transmit * survive * shaded - later) / RAY_DEPTH_CELLS
    grad_colors = image_grad[:, None] * weight[None]
    render_grad = jnp.concatenate([grad_density[None], grad_colors], axis=0)
    tv_grad = tv_along(grid_values, 1) + tv_along(grid_values, 2) + tv_along(grid_values, 3)
    return render_grad + TV_WEIGHT * tv_grad
```

```python
import jax
import jax.numpy as jnp
from jax import lax
from jax.experimental import pallas as pl
from jax.experimental.pallas import tpu as pltpu
from jax.sharding import PartitionSpec as P

SMOOTH = 0.01
TV_WEIGHT = 0.05
MESH = pl.DeviceIdType.MESH
C, Z, R, W = 4, 32, 8, 512
D = 8
CELLS = 256


def slope_of(d):
    return d * lax.rsqrt(d * d + SMOOTH)


def kernel(
    ig_ref, g_hbm, out,
    g, igs, opt, lig, lw, tn, lo_src, hi_src, from_prev, from_next, z_prev, z_next,
    in_sem, ig_send, ig_recv, op_send, op_recv, li_send, li_recv,
    row_send, row_recv, z_send, z_recv,
):
    rows_n = lax.axis_size("rows")
    rp = lax.axis_index("rows")
    me = lax.axis_index("depth")
    r_up, r_down = lax.rem(rp + 1, rows_n), lax.rem(rp + rows_n - 1, rows_n)
    peers = [(rp, lax.rem(me + k, D)) for k in range(1, D)]

    barrier = pltpu.get_barrier_semaphore()
    for dev in peers + [(r_up, me), (r_down, me)]:
        pl.semaphore_signal(barrier, inc=1, device_id=dev, device_id_type=MESH)
    loads = [pltpu.make_async_copy(g_hbm.at[c], g.at[c], in_sem.at[c]) for c in range(C)]
    for cp in loads:
        cp.start()

    def remote(src, dst, send, recv, dev):
        return pltpu.make_async_remote_copy(
            src_ref=src, dst_ref=dst, send_sem=send, recv_sem=recv,
            device_id=dev, device_id_type=MESH,
        )

    igs[0] = ig_ref[...]
    pl.semaphore_wait(barrier, D + 1)
    sent = []
    ig_cp = [
        remote(ig_ref, igs.at[k], ig_send.at[k], ig_recv.at[k], peers[k - 1])
        for k in range(1, D)
    ]
    for cp in ig_cp:
        cp.start()

    row_cp = []
    for c in range(C):
        loads[c].wait()

        def pack(z, _, c=c):
            lo_src[c, pl.ds(z, 1), :] = g[c, z, 0:1, :]
            hi_src[c, pl.ds(z, 1), :] = g[c, z, R - 1:R, :]
            return 0

        lax.fori_loop(0, Z, pack, 0, unroll=8)
        up = remote(hi_src.at[c], from_prev.at[c], row_send.at[0, c], row_recv.at[0, c], (r_up, me))
        down = remote(lo_src.at[c], from_next.at[c], row_send.at[1, c], row_recv.at[1, c], (r_down, me))
        up.start()
        down.start()
        row_cp += [up, down]

    def march(z, carry):
        before = carry
        o = g[0, z] * (1.0 / CELLS)
        s = jnp.exp(-o)
        t = jnp.exp(-before)
        lw[z] = t * (1.0 - s)
        tn[z] = t * s
        return before + o

    opt[0] = lax.fori_loop(0, Z, march, jnp.zeros((R, W), jnp.float32), unroll=4)
    op_cp = [
        remote(opt.at[0], opt.at[k], op_send.at[k], op_recv.at[k], peers[k - 1])
        for k in range(1, D)
    ]
    for cp in op_cp:
        cp.start()

    z_cp = [
        remote(g.at[:, Z - 1], z_prev, z_send.at[0], z_recv.at[0], (rp, lax.rem(me + 1, D))),
        remote(g.at[:, 0], z_next, z_send.at[1], z_recv.at[1], (rp, lax.rem(me + D - 1, D))),
    ]

    for cp in ig_cp:
        cp.wait_recv()
    parts = [igs[lax.rem(me - d + D, D)] for d in range(D)]
    grad = jnp.concatenate(parts, axis=-1)

    def light(i, later):
        z = Z - 1 - i
        shaded = grad[0] * g[1, z] + grad[1] * g[2, z] + grad[2] * g[3, z]
        tn[z] = (tn[z] * shaded - later) * (1.0 / CELLS)
        return later + lw[z] * shaded

    lig[0] = lax.fori_loop(0, Z, light, jnp.zeros((R, W), jnp.float32), unroll=2)
    li_cp = [
        remote(lig.at[0], lig.at[k], li_send.at[k], li_recv.at[k], peers[k - 1])
        for k in range(1, D)
    ]
    for cp in li_cp:
        cp.start()
    for cp in z_cp:
        cp.start()

    col0 = lax.broadcasted_iota(jnp.int32, (R, W), 1) == 0
    row0 = lax.broadcasted_iota(jnp.int32, (R, W), 0) == 0
    zero = jnp.zeros((R, W), jnp.float32)

    def plane_tv(t):
        dc = jnp.where(col0, 0.0, t - pltpu.roll(t, 1, 1))
        sc = slope_of(dc)
        dr = jnp.where(row0, 0.0, t - pltpu.roll(t, 1, 0))
        sr = slope_of(dr)
        return (sc - pltpu.roll(sc, W - 1, 1)) + (sr - pltpu.roll(sr, R - 1, 0))

    for c in range(C):
        def tv(z, carry, c=c):
            t, s_lo = carry
            nxt = g[c, z + 1]
            s_hi = slope_of(nxt - t)
            out[c, z] = TV_WEIGHT * (plane_tv(t) + (s_lo - s_hi))
            return nxt, s_hi

        t, s_lo = lax.fori_loop(0, Z - 1, tv, (g[c, 0], zero))
        out[c, Z - 1] = TV_WEIGHT * (plane_tv(t) + s_lo)

    for cp in op_cp + li_cp:
        cp.wait_recv()
    passed, beyond, entering = zero, zero, zero
    for d in range(D):
        k = lax.rem(me - d + D, D)
        enter_d = jnp.exp(-passed)
        entering = jnp.where(me == d, enter_d, entering)
        beyond = beyond + jnp.where(me < d, enter_d * lig[k], 0.0)
        passed = passed + opt[k]
    beyond = beyond * (1.0 / CELLS)
    coeff = [grad[j] * entering for j in range(3)]

    def render(z, _):
        out[0, z] = out[0, z] + (entering * tn[z] - beyond)
        w = lw[z]
        for j in range(3):
            out[1 + j, z] = out[1 + j, z] + coeff[j] * w
        return 0

    lax.fori_loop(0, Z, render, 0, unroll=2)

    for cp in z_cp:
        cp.wait_recv()
    for c in range(C):
        lo = slope_of(g[c, 0] - z_prev[c])
        hi = slope_of(z_next[c] - g[c, Z - 1])
        out[c, 0] = out[c, 0] + jnp.where(me > 0, TV_WEIGHT * lo, 0.0)
        out[c, Z - 1] = out[c, Z - 1] - jnp.where(me < D - 1, TV_WEIGHT * hi, 0.0)
    for c in range(C):
        row_cp[2 * c].wait()
        row_cp[2 * c + 1].wait()
        lo = slope_of(lo_src[c] - from_prev[c])
        hi = slope_of(from_next[c] - hi_src[c])
        from_prev[c] = jnp.where(rp > 0, TV_WEIGHT * lo, 0.0)
        from_next[c] = jnp.where(rp < rows_n - 1, TV_WEIGHT * hi, 0.0)

        def fix(z, _, c=c):
            out[c, z, 0:1, :] = out[c, z, 0:1, :] + from_prev[c, pl.ds(z, 1), :]
            out[c, z, R - 1:R, :] = out[c, z, R - 1:R, :] - from_next[c, pl.ds(z, 1), :]
            return 0

        lax.fori_loop(0, Z, fix, 0, unroll=8)

    for cp in ig_cp + op_cp + li_cp + z_cp:
        cp.wait_send()


def shards(grid_values, image_grad):
    f32 = jnp.float32
    dma = pltpu.SemaphoreType.DMA
    return pl.pallas_call(
        kernel,
        out_shape=jax.ShapeDtypeStruct((C, Z, R, W), f32),
        in_specs=[
            pl.BlockSpec(memory_space=pltpu.VMEM),
            pl.BlockSpec(memory_space=pl.ANY),
        ],
        out_specs=pl.BlockSpec(memory_space=pltpu.VMEM),
        scratch_shapes=[
            pltpu.VMEM((C, Z, R, W), f32),
            pltpu.VMEM((D, 3, R, W // D), f32),
            pltpu.VMEM((D, R, W), f32),
            pltpu.VMEM((D, R, W), f32),
            pltpu.VMEM((Z, R, W), f32),
            pltpu.VMEM((Z, R, W), f32),
            pltpu.VMEM((C, Z, W), f32),
            pltpu.VMEM((C, Z, W), f32),
            pltpu.VMEM((C, Z, W), f32),
            pltpu.VMEM((C, Z, W), f32),
            pltpu.VMEM((C, R, W), f32),
            pltpu.VMEM((C, R, W), f32),
            dma((C,)),
            dma((D,)), dma((D,)), dma((D,)), dma((D,)), dma((D,)), dma((D,)),
            dma((2, C)), dma((2, C)), dma((2,)), dma((2,)),
        ],
        compiler_params=pltpu.CompilerParams(collective_id=0, has_side_effects=True),
        name="render_adjoint",
    )(image_grad, grid_values)


def solution(mesh):
    return jax.shard_map(
        shards,
        mesh=mesh,
        in_specs=(P(None, "depth", "rows", None), P(None, "rows", "depth")),
        out_specs=P(None, "depth", "rows", None),
        check_vma=False,
    )
```

```python
import jax
import jax.numpy as jnp
from jax import lax
from jax.experimental import pallas as pl
from jax.experimental.pallas import tpu as pltpu
from jax.sharding import PartitionSpec as P

SMOOTH = 0.01
TV_WEIGHT = 0.05
MESH = pl.DeviceIdType.MESH
C, Z, R, W = 4, 32, 8, 512
D = 8
CELLS = 256


def slope_of(d):
    return d * lax.rsqrt(d * d + SMOOTH)


def kernel(
    ig_ref, g_hbm, out,
    g, igs, opt, lig, lw, tn, lo_src, hi_src, from_prev, from_next, z_prev, z_next,
    in_sem, ig_send, ig_recv, op_send, op_recv, li_send, li_recv,
    row_send, row_recv, z_send, z_recv,
):
    rows_n = lax.axis_size("rows")
    rp = lax.axis_index("rows")
    me = lax.axis_index("depth")
    r_up, r_down = lax.rem(rp + 1, rows_n), lax.rem(rp + rows_n - 1, rows_n)
    peers = [(rp, lax.rem(me + k, D)) for k in range(1, D)]

    barrier = pltpu.get_barrier_semaphore()
    for dev in peers + [(r_up, me), (r_down, me)]:
        pl.semaphore_signal(barrier, inc=1, device_id=dev, device_id_type=MESH)
    loads = [pltpu.make_async_copy(g_hbm.at[c], g.at[c], in_sem.at[c]) for c in range(C)]
    for cp in loads:
        cp.start()

    def remote(src, dst, send, recv, dev):
        return pltpu.make_async_remote_copy(
            src_ref=src, dst_ref=dst, send_sem=send, recv_sem=recv,
            device_id=dev, device_id_type=MESH,
        )

    igs[0] = ig_ref[...]
    pl.semaphore_wait(barrier, D + 1)
    sent = []
    ig_cp = [
        remote(ig_ref, igs.at[k], ig_send.at[k], ig_recv.at[k], peers[k - 1])
        for k in range(1, D)
    ]
    for cp in ig_cp:
        cp.start()

    row_cp = []
    for c in range(C):
        loads[c].wait()

        def pack(z, _, c=c):
            lo_src[c, pl.ds(z, 1), :] = g[c, z, 0:1, :]
            hi_src[c, pl.ds(z, 1), :] = g[c, z, R - 1:R, :]
            return 0

        lax.fori_loop(0, Z, pack, 0, unroll=16)
        up = remote(hi_src.at[c], from_prev.at[c], row_send.at[0, c], row_recv.at[0, c], (r_up, me))
        down = remote(lo_src.at[c], from_next.at[c], row_send.at[1, c], row_recv.at[1, c], (r_down, me))
        up.start()
        down.start()
        row_cp += [up, down]

    def march(z, carry):
        before = carry
        o = g[0, z] * (1.0 / CELLS)
        s = jnp.exp(-o)
        t = jnp.exp(-before)
        lw[z] = t * (1.0 - s)
        tn[z] = t * s
        return before + o

    opt[0] = lax.fori_loop(0, Z, march, jnp.zeros((R, W), jnp.float32), unroll=8)
    op_cp = [
        remote(opt.at[0], opt.at[k], op_send.at[k], op_recv.at[k], peers[k - 1])
        for k in range(1, D)
    ]
    for cp in op_cp:
        cp.start()

    z_cp = [
        remote(g.at[:, Z - 1], z_prev, z_send.at[0], z_recv.at[0], (rp, lax.rem(me + 1, D))),
        remote(g.at[:, 0], z_next, z_send.at[1], z_recv.at[1], (rp, lax.rem(me + D - 1, D))),
    ]

    for cp in z_cp:
        cp.start()

    for cp in ig_cp:
        cp.wait_recv()
    parts = [igs[lax.rem(me - d + D, D)] for d in range(D)]
    grad = jnp.concatenate(parts, axis=-1)

    def light(i, later):
        z = Z - 1 - i
        shaded = grad[0] * g[1, z] + grad[1] * g[2, z] + grad[2] * g[3, z]
        tn[z] = (tn[z] * shaded - later) * (1.0 / CELLS)
        return later + lw[z] * shaded

    lig[0] = lax.fori_loop(0, Z, light, jnp.zeros((R, W), jnp.float32), unroll=8)
    li_cp = [
        remote(lig.at[0], lig.at[k], li_send.at[k], li_recv.at[k], peers[k - 1])
        for k in range(1, D)
    ]
    for cp in li_cp:
        cp.start()

    col0 = lax.broadcasted_iota(jnp.int32, (R, W), 1) == 0
    row0 = lax.broadcasted_iota(jnp.int32, (R, W), 0) == 0
    zero = jnp.zeros((R, W), jnp.float32)

    def plane_tv(t):
        dc = jnp.where(col0, 0.0, t - pltpu.roll(t, 1, 1))
        sc = slope_of(dc)
        dr = jnp.where(row0, 0.0, t - pltpu.roll(t, 1, 0))
        sr = slope_of(dr)
        return (sc - pltpu.roll(sc, W - 1, 1)) + (sr - pltpu.roll(sr, R - 1, 0))

    for c in range(C):
        def tv(z, carry, c=c):
            t, s_lo = carry
            nxt = g[c, jnp.minimum(z + 1, Z - 1)]
            s_hi = slope_of(nxt - t)
            out[c, z] = TV_WEIGHT * (plane_tv(t) + (s_lo - s_hi))
            return nxt, s_hi

        lax.fori_loop(0, Z, tv, (g[c, 0], zero), unroll=8)

    for cp in op_cp + li_cp:
        cp.wait_recv()
    passed, beyond, entering = zero, zero, zero
    for d in range(D):
        k = lax.rem(me - d + D, D)
        enter_d = jnp.exp(-passed)
        entering = jnp.where(me == d, enter_d, entering)
        beyond = beyond + jnp.where(me < d, enter_d * lig[k], 0.0)
        passed = passed + opt[k]
    beyond = beyond * (1.0 / CELLS)
    coeff = [grad[j] * entering for j in range(3)]

    def render(z, _):
        out[0, z] = out[0, z] + (entering * tn[z] - beyond)
        w = lw[z]
        for j in range(3):
            out[1 + j, z] = out[1 + j, z] + coeff[j] * w
        return 0

    lax.fori_loop(0, Z, render, 0, unroll=4)

    for cp in z_cp:
        cp.wait_recv()
    for c in range(C):
        lo = slope_of(g[c, 0] - z_prev[c])
        hi = slope_of(z_next[c] - g[c, Z - 1])
        out[c, 0] = out[c, 0] + jnp.where(me > 0, TV_WEIGHT * lo, 0.0)
        out[c, Z - 1] = out[c, Z - 1] - jnp.where(me < D - 1, TV_WEIGHT * hi, 0.0)
    for c in range(C):
        row_cp[2 * c].wait()
        row_cp[2 * c + 1].wait()
        lo = slope_of(lo_src[c] - from_prev[c])
        hi = slope_of(from_next[c] - hi_src[c])
        from_prev[c] = jnp.where(rp > 0, TV_WEIGHT * lo, 0.0)
        from_next[c] = jnp.where(rp < rows_n - 1, TV_WEIGHT * hi, 0.0)

        def fix(z, _, c=c):
            out[c, z, 0:1, :] = out[c, z, 0:1, :] + from_prev[c, pl.ds(z, 1), :]
            out[c, z, R - 1:R, :] = out[c, z, R - 1:R, :] - from_next[c, pl.ds(z, 1), :]
            return 0

        lax.fori_loop(0, Z, fix, 0, unroll=16)

    for cp in ig_cp + op_cp + li_cp + z_cp:
        cp.wait_send()


def shards(grid_values, image_grad):
    f32 = jnp.float32
    dma = pltpu.SemaphoreType.DMA
    return pl.pallas_call(
        kernel,
        out_shape=pltpu.MemorySpace.VMEM((C, Z, R, W), f32),
        in_specs=[
            pl.BlockSpec(memory_space=pltpu.VMEM),
            pl.BlockSpec(memory_space=pl.ANY),
        ],
        out_specs=pl.BlockSpec(memory_space=pltpu.VMEM),
        scratch_shapes=[
            pltpu.VMEM((C, Z, R, W), f32),
            pltpu.VMEM((D, 3, R, W // D), f32),
            pltpu.VMEM((D, R, W), f32),
            pltpu.VMEM((D, R, W), f32),
            pltpu.VMEM((Z, R, W), f32),
            pltpu.VMEM((Z, R, W), f32),
            pltpu.VMEM((C, Z, W), f32),
            pltpu.VMEM((C, Z, W), f32),
            pltpu.VMEM((C, Z, W), f32),
            pltpu.VMEM((C, Z, W), f32),
            pltpu.VMEM((C, R, W), f32),
            pltpu.VMEM((C, R, W), f32),
            dma((C,)),
            dma((D,)), dma((D,)), dma((D,)), dma((D,)), dma((D,)), dma((D,)),
            dma((2, C)), dma((2, C)), dma((2,)), dma((2,)),
        ],
        compiler_params=pltpu.CompilerParams(collective_id=0, has_side_effects=True),
        name="render_adjoint",
    )(image_grad, grid_values)


def solution(mesh):
    return jax.shard_map(
        shards,
        mesh=mesh,
        in_specs=(P(None, "depth", "rows", None), P(None, "rows", "depth")),
        out_specs=P(None, "depth", "rows", None),
        check_vma=False,
    )
```

```python
import jax
import jax.numpy as jnp
from jax import lax
from jax.experimental import pallas as pl
from jax.experimental.pallas import tpu as pltpu
from jax.sharding import PartitionSpec as P

SMOOTH = 0.01
TV_WEIGHT = 0.05
MESH = pl.DeviceIdType.MESH
C, Z, R, W = 4, 32, 8, 512
D = 8
CELLS = 256


def slope_of(d):
    return d * lax.rsqrt(d * d + SMOOTH)


def kernel(
    ig_ref, g_hbm, out,
    g, igs, opt, lig, lw, tn, lo_src, hi_src, from_prev, from_next, z_prev, z_next,
    in_sem, ig_send, ig_recv, op_send, op_recv, li_send, li_recv,
    row_send, row_recv, z_send, z_recv,
):
    rows_n = lax.axis_size("rows")
    rp = lax.axis_index("rows")
    me = lax.axis_index("depth")
    r_up, r_down = lax.rem(rp + 1, rows_n), lax.rem(rp + rows_n - 1, rows_n)
    peers = [(rp, lax.rem(me + k, D)) for k in range(1, D)]

    barrier = pltpu.get_barrier_semaphore()
    for dev in peers + [(r_up, me), (r_down, me)]:
        pl.semaphore_signal(barrier, inc=1, device_id=dev, device_id_type=MESH)
    loads = [pltpu.make_async_copy(g_hbm.at[c], g.at[c], in_sem.at[c]) for c in range(C)]
    for cp in loads:
        cp.start()

    def remote(src, dst, send, recv, dev):
        return pltpu.make_async_remote_copy(
            src_ref=src, dst_ref=dst, send_sem=send, recv_sem=recv,
            device_id=dev, device_id_type=MESH,
        )

    igs[0] = ig_ref[...]
    pl.semaphore_wait(barrier, D + 1)
    ig_cp = [
        remote(ig_ref, igs.at[k], ig_send.at[k], ig_recv.at[k], peers[k - 1])
        for k in range(1, D)
    ]
    for cp in ig_cp:
        cp.start()

    row_cp = []
    for c in range(C):
        up = remote(g_hbm.at[c, :, R - 1], from_prev.at[c], row_send.at[0, c], row_recv.at[0, c], (r_up, me))
        down = remote(g_hbm.at[c, :, 0], from_next.at[c], row_send.at[1, c], row_recv.at[1, c], (r_down, me))
        up.start()
        down.start()
        row_cp += [up, down]
    loads[0].wait()

    def march(z, carry):
        before = carry
        o = g[0, z] * (1.0 / CELLS)
        s = jnp.exp(-o)
        t = jnp.exp(-before)
        lw[z] = t * (1.0 - s)
        tn[z] = t * s
        return before + o

    opt[0] = lax.fori_loop(0, Z, march, jnp.zeros((R, W), jnp.float32), unroll=8)
    op_cp = [
        remote(opt.at[0], opt.at[k], op_send.at[k], op_recv.at[k], peers[k - 1])
        for k in range(1, D)
    ]
    for cp in op_cp:
        cp.start()

    for c in range(1, C):
        loads[c].wait()
    z_cp = [
        remote(g.at[:, Z - 1], z_prev, z_send.at[0], z_recv.at[0], (rp, lax.rem(me + 1, D))),
        remote(g.at[:, 0], z_next, z_send.at[1], z_recv.at[1], (rp, lax.rem(me + D - 1, D))),
    ]

    for cp in z_cp:
        cp.start()

    col0 = lax.broadcasted_iota(jnp.int32, (R, W), 1) == 0
    row0 = lax.broadcasted_iota(jnp.int32, (R, W), 0) == 0
    zero = jnp.zeros((R, W), jnp.float32)

    def plane_tv(t):
        dc = jnp.where(col0, 0.0, t - pltpu.roll(t, 1, 1))
        sc = slope_of(dc)
        dr = jnp.where(row0, 0.0, t - pltpu.roll(t, 1, 0))
        sr = slope_of(dr)
        return (sc - pltpu.roll(sc, W - 1, 1)) + (sr - pltpu.roll(sr, R - 1, 0))

    def inner_tv(c):
        def tv(z, carry):
            t, s_lo = carry
            nxt = g[c, jnp.minimum(z + 1, Z - 1)]
            s_hi = slope_of(nxt - t)
            out[c, z] = TV_WEIGHT * (plane_tv(t) + (s_lo - s_hi))
            return nxt, s_hi

        lax.fori_loop(0, Z, tv, (g[c, 0], zero), unroll=8)

    for c in range(2):
        inner_tv(c)

    for cp in ig_cp:
        cp.wait_recv()
    parts = [igs[lax.rem(me - d + D, D)] for d in range(D)]
    grad = jnp.concatenate(parts, axis=-1)

    def light(i, later):
        z = Z - 1 - i
        shaded = grad[0] * g[1, z] + grad[1] * g[2, z] + grad[2] * g[3, z]
        tn[z] = (tn[z] * shaded - later) * (1.0 / CELLS)
        return later + lw[z] * shaded

    lig[0] = lax.fori_loop(0, Z, light, jnp.zeros((R, W), jnp.float32), unroll=8)
    li_cp = [
        remote(lig.at[0], lig.at[k], li_send.at[k], li_recv.at[k], peers[k - 1])
        for k in range(1, D)
    ]
    for k in range(1, D):
        @pl.when(me + k >= D)
        def _(k=k):
            li_cp[k - 1].start()


    for c in range(C):

        def pack(z, _, c=c):
            lo_src[c, pl.ds(z, 1), :] = g[c, z, 0:1, :]
            hi_src[c, pl.ds(z, 1), :] = g[c, z, R - 1:R, :]
            return 0

        lax.fori_loop(0, Z, pack, 0, unroll=16)

    for c in range(2, C):
        inner_tv(c)

    for cp in op_cp:
        cp.wait_recv()
    for k in range(1, D):
        @pl.when(me - k < 0)
        def _(k=k):
            li_cp[k - 1].wait_recv()

    passed, beyond, entering = zero, zero, zero
    for d in range(D):
        k = lax.rem(me - d + D, D)
        enter_d = jnp.exp(-passed)
        entering = jnp.where(me == d, enter_d, entering)
        beyond = beyond + jnp.where(me < d, enter_d * lig[k], 0.0)
        passed = passed + opt[k]
    beyond = beyond * (1.0 / CELLS)
    coeff = [grad[j] * entering for j in range(3)]

    def render(z, _):
        out[0, z] = out[0, z] + (entering * tn[z] - beyond)
        w = lw[z]
        for j in range(3):
            out[1 + j, z] = out[1 + j, z] + coeff[j] * w
        return 0

    lax.fori_loop(0, Z, render, 0, unroll=4)

    for cp in z_cp:
        cp.wait_recv()
    for c in range(C):
        lo = slope_of(g[c, 0] - z_prev[c])
        hi = slope_of(z_next[c] - g[c, Z - 1])
        out[c, 0] = out[c, 0] + jnp.where(me > 0, TV_WEIGHT * lo, 0.0)
        out[c, Z - 1] = out[c, Z - 1] - jnp.where(me < D - 1, TV_WEIGHT * hi, 0.0)
    for c in range(C):
        row_cp[2 * c].wait()
        row_cp[2 * c + 1].wait()
        lo = slope_of(lo_src[c] - from_prev[c])
        hi = slope_of(from_next[c] - hi_src[c])
        from_prev[c] = jnp.where(rp > 0, TV_WEIGHT * lo, 0.0)
        from_next[c] = jnp.where(rp < rows_n - 1, TV_WEIGHT * hi, 0.0)

        def fix(z, _, c=c):
            out[c, z, 0:1, :] = out[c, z, 0:1, :] + from_prev[c, pl.ds(z, 1), :]
            out[c, z, R - 1:R, :] = out[c, z, R - 1:R, :] - from_next[c, pl.ds(z, 1), :]
            return 0

        lax.fori_loop(0, Z, fix, 0, unroll=16)

    for cp in ig_cp + op_cp + z_cp:
        cp.wait_send()
    for k in range(1, D):
        @pl.when(me + k >= D)
        def _(k=k):
            li_cp[k - 1].wait_send()


def shards(grid_values, image_grad):
    f32 = jnp.float32
    dma = pltpu.SemaphoreType.DMA
    return pl.pallas_call(
        kernel,
        out_shape=pltpu.MemorySpace.VMEM((C, Z, R, W), f32),
        in_specs=[
            pl.BlockSpec(memory_space=pltpu.VMEM),
            pl.BlockSpec(memory_space=pl.ANY),
        ],
        out_specs=pl.BlockSpec(memory_space=pltpu.VMEM),
        scratch_shapes=[
            pltpu.VMEM((C, Z, R, W), f32),
            pltpu.VMEM((D, 3, R, W // D), f32),
            pltpu.VMEM((D, R, W), f32),
            pltpu.VMEM((D, R, W), f32),
            pltpu.VMEM((Z, R, W), f32),
            pltpu.VMEM((Z, R, W), f32),
            pltpu.VMEM((C, Z, W), f32),
            pltpu.VMEM((C, Z, W), f32),
            pltpu.VMEM((C, Z, W), f32),
            pltpu.VMEM((C, Z, W), f32),
            pltpu.VMEM((C, R, W), f32),
            pltpu.VMEM((C, R, W), f32),
            dma((C,)),
            dma((D,)), dma((D,)), dma((D,)), dma((D,)), dma((D,)), dma((D,)),
            dma((2, C)), dma((2, C)), dma((2,)), dma((2,)),
        ],
        compiler_params=pltpu.CompilerParams(collective_id=0, has_side_effects=True),
        name="render_adjoint",
    )(image_grad, grid_values)


def solution(mesh):
    return jax.shard_map(
        shards,
        mesh=mesh,
        in_specs=(P(None, "depth", "rows", None), P(None, "rows", "depth")),
        out_specs=P(None, "depth", "rows", None),
        check_vma=False,
    )
```

```python
import jax
import jax.numpy as jnp
from jax import lax
from jax.experimental import pallas as pl
from jax.experimental.pallas import tpu as pltpu
from jax.sharding import PartitionSpec as P

SMOOTH = 0.01
TV_WEIGHT = 0.05
MESH = pl.DeviceIdType.MESH
C, Z, R, W = 4, 32, 8, 512
D = 8
CELLS = 256


def slope_of(d):
    return d * lax.rsqrt(d * d + SMOOTH)


def kernel(
    ig_ref, g_hbm, out,
    g, igs, opt, lig, lw, tn, lo_src, hi_src, from_prev, from_next, z_prev, z_next,
    in_sem, ig_send, ig_recv, op_send, op_recv, li_send, li_recv,
    row_send, row_recv, z_send, z_recv,
):
    rows_n = lax.axis_size("rows")
    rp = lax.axis_index("rows")
    me = lax.axis_index("depth")
    r_up, r_down = lax.rem(rp + 1, rows_n), lax.rem(rp + rows_n - 1, rows_n)
    peers = [(rp, lax.rem(me + k, D)) for k in range(1, D)]

    barrier = pltpu.get_barrier_semaphore()
    for dev in peers + [(r_up, me), (r_down, me)]:
        pl.semaphore_signal(barrier, inc=1, device_id=dev, device_id_type=MESH)
    loads = [pltpu.make_async_copy(g_hbm.at[c], g.at[c], in_sem.at[c]) for c in range(C)]
    for cp in loads:
        cp.start()

    def remote(src, dst, send, recv, dev):
        return pltpu.make_async_remote_copy(
            src_ref=src, dst_ref=dst, send_sem=send, recv_sem=recv,
            device_id=dev, device_id_type=MESH,
        )

    igs[0] = ig_ref[...]
    pl.semaphore_wait(barrier, D + 1)
    ig_cp = [
        remote(ig_ref, igs.at[k], ig_send.at[k], ig_recv.at[k], peers[k - 1])
        for k in range(1, D)
    ]
    for cp in ig_cp:
        cp.start()

    z_cp = [
        remote(g_hbm.at[:, Z - 1], z_prev, z_send.at[0], z_recv.at[0], (rp, lax.rem(me + 1, D))),
        remote(g_hbm.at[:, 0], z_next, z_send.at[1], z_recv.at[1], (rp, lax.rem(me + D - 1, D))),
    ]
    for cp in z_cp:
        cp.start()

    row_cp = []
    for c in range(C):
        up = remote(g_hbm.at[c, :, R - 1], from_prev.at[c], row_send.at[0, c], row_recv.at[0, c], (r_up, me))
        down = remote(g_hbm.at[c, :, 0], from_next.at[c], row_send.at[1, c], row_recv.at[1, c], (r_down, me))
        up.start()
        down.start()
        row_cp += [up, down]
    loads[0].wait()

    def march(z, carry):
        before = carry
        o = g[0, z] * (1.0 / CELLS)
        s = jnp.exp(-o)
        t = jnp.exp(-before)
        lw[z] = t * (1.0 - s)
        tn[z] = t * s
        return before + o

    opt[0] = lax.fori_loop(0, Z, march, jnp.zeros((R, W), jnp.float32), unroll=8)
    op_cp = [
        remote(opt.at[0], opt.at[k], op_send.at[k], op_recv.at[k], peers[k - 1])
        for k in range(1, D)
    ]
    for cp in op_cp:
        cp.start()

    for c in range(1, C):
        loads[c].wait()


    col0 = lax.broadcasted_iota(jnp.int32, (R, W), 1) == 0
    row0 = lax.broadcasted_iota(jnp.int32, (R, W), 0) == 0
    zero = jnp.zeros((R, W), jnp.float32)

    def plane_tv(t):
        dc = jnp.where(col0, 0.0, t - pltpu.roll(t, 1, 1))
        sc = slope_of(dc)
        dr = jnp.where(row0, 0.0, t - pltpu.roll(t, 1, 0))
        sr = slope_of(dr)
        return (sc - pltpu.roll(sc, W - 1, 1)) + (sr - pltpu.roll(sr, R - 1, 0))

    def inner_tv(c):
        def tv(z, carry):
            t, s_lo = carry
            nxt = g[c, jnp.minimum(z + 1, Z - 1)]
            s_hi = slope_of(nxt - t)
            out[c, z] = TV_WEIGHT * (plane_tv(t) + (s_lo - s_hi))
            return nxt, s_hi

        lax.fori_loop(0, Z, tv, (g[c, 0], zero), unroll=8)

    for c in range(1):
        inner_tv(c)

    for cp in ig_cp:
        cp.wait_recv()
    parts = [igs[lax.rem(me - d + D, D)] for d in range(D)]
    grad = jnp.concatenate(parts, axis=-1)

    def light(i, later):
        z = Z - 1 - i
        shaded = grad[0] * g[1, z] + grad[1] * g[2, z] + grad[2] * g[3, z]
        tn[z] = (tn[z] * shaded - later) * (1.0 / CELLS)
        return later + lw[z] * shaded

    lig[0] = lax.fori_loop(0, Z, light, jnp.zeros((R, W), jnp.float32), unroll=8)
    li_cp = [
        remote(lig.at[0], lig.at[k], li_send.at[k], li_recv.at[k], peers[k - 1])
        for k in range(1, D)
    ]
    for k in range(1, D):
        @pl.when(me + k >= D)
        def _(k=k):
            li_cp[k - 1].start()


    for c in range(C):

        def pack(z, _, c=c):
            lo_src[c, pl.ds(z, 1), :] = g[c, z, 0:1, :]
            hi_src[c, pl.ds(z, 1), :] = g[c, z, R - 1:R, :]
            return 0

        lax.fori_loop(0, Z, pack, 0, unroll=16)

    for c in range(1, C):
        inner_tv(c)

    for cp in op_cp:
        cp.wait_recv()
    for k in range(1, D):
        @pl.when(me - k < 0)
        def _(k=k):
            li_cp[k - 1].wait_recv()

    passed, beyond, entering = zero, zero, zero
    for d in range(D):
        k = lax.rem(me - d + D, D)
        enter_d = jnp.exp(-passed)
        entering = jnp.where(me == d, enter_d, entering)
        beyond = beyond + jnp.where(me < d, enter_d * lig[k], 0.0)
        passed = passed + opt[k]
    beyond = beyond * (1.0 / CELLS)
    coeff = [grad[j] * entering for j in range(3)]

    def render(z, _):
        out[0, z] = out[0, z] + (entering * tn[z] - beyond)
        w = lw[z]
        for j in range(3):
            out[1 + j, z] = out[1 + j, z] + coeff[j] * w
        return 0

    lax.fori_loop(0, Z, render, 0, unroll=4)

    for cp in z_cp:
        cp.wait_recv()
    for c in range(C):
        lo = slope_of(g[c, 0] - z_prev[c])
        hi = slope_of(z_next[c] - g[c, Z - 1])
        out[c, 0] = out[c, 0] + jnp.where(me > 0, TV_WEIGHT * lo, 0.0)
        out[c, Z - 1] = out[c, Z - 1] - jnp.where(me < D - 1, TV_WEIGHT * hi, 0.0)
    for c in range(C):
        row_cp[2 * c].wait()
        row_cp[2 * c + 1].wait()
        lo = slope_of(lo_src[c] - from_prev[c])
        hi = slope_of(from_next[c] - hi_src[c])
        from_prev[c] = jnp.where(rp > 0, TV_WEIGHT * lo, 0.0)
        from_next[c] = jnp.where(rp < rows_n - 1, TV_WEIGHT * hi, 0.0)

        def fix(z, _, c=c):
            out[c, z, 0:1, :] = out[c, z, 0:1, :] + from_prev[c, pl.ds(z, 1), :]
            out[c, z, R - 1:R, :] = out[c, z, R - 1:R, :] - from_next[c, pl.ds(z, 1), :]
            return 0

        lax.fori_loop(0, Z, fix, 0, unroll=16)

    for cp in ig_cp + op_cp + z_cp:
        cp.wait_send()
    for k in range(1, D):
        @pl.when(me + k >= D)
        def _(k=k):
            li_cp[k - 1].wait_send()


def shards(grid_values, image_grad):
    f32 = jnp.float32
    dma = pltpu.SemaphoreType.DMA
    return pl.pallas_call(
        kernel,
        out_shape=pltpu.MemorySpace.VMEM((C, Z, R, W), f32),
        in_specs=[
            pl.BlockSpec(memory_space=pltpu.VMEM),
            pl.BlockSpec(memory_space=pl.ANY),
        ],
        out_specs=pl.BlockSpec(memory_space=pltpu.VMEM),
        scratch_shapes=[
            pltpu.VMEM((C, Z, R, W), f32),
            pltpu.VMEM((D, 3, R, W // D), f32),
            pltpu.VMEM((D, R, W), f32),
            pltpu.VMEM((D, R, W), f32),
            pltpu.VMEM((Z, R, W), f32),
            pltpu.VMEM((Z, R, W), f32),
            pltpu.VMEM((C, Z, W), f32),
            pltpu.VMEM((C, Z, W), f32),
            pltpu.VMEM((C, Z, W), f32),
            pltpu.VMEM((C, Z, W), f32),
            pltpu.VMEM((C, R, W), f32),
            pltpu.VMEM((C, R, W), f32),
            dma((C,)),
            dma((D,)), dma((D,)), dma((D,)), dma((D,)), dma((D,)), dma((D,)),
            dma((2, C)), dma((2, C)), dma((2,)), dma((2,)),
        ],
        compiler_params=pltpu.CompilerParams(collective_id=0, has_side_effects=True),
        name="render_adjoint",
    )(image_grad, grid_values)


def solution(mesh):
    return jax.shard_map(
        shards,
        mesh=mesh,
        in_specs=(P(None, "depth", "rows", None), P(None, "rows", "depth")),
        out_specs=P(None, "depth", "rows", None),
        check_vma=False,
    )
```
